32 devices in a mesh: shard: 2 (over x), tensor: 4 (over y, core), section: 4 (over z).
Axes of the slice: x: 2, y: 2, z: 4, core: 2. Of those that a mesh axis runs over, the one named last changes fastest.
Arguments:
- grad_kv: bfloat16 [16, 1024, 2048], P(('shard', 'section'), None, 'tensor'), may hold values from -65000 to 65000
- grad_gate: bfloat16 [16, 512, 2048], P(('shard', 'section'), None, 'tensor'), may hold values from -65000 to 65000
- grad_laurel: bfloat16 [16, 128, 2048], P(('shard', 'section'), None, 'tensor'), may hold values from -65000 to 65000
- master_kv: float32 [1024, 2048], P(('shard', 'section'), 'tensor'), may hold values from -0.1 to 0.1
- master_gate: float32 [512, 2048], P(('shard', 'section'), 'tensor'), may hold values from -0.1 to 0.1
- master_laurel: float32 [128, 2048], P(('shard', 'section'), 'tensor'), may hold values from -0.1 to 0.1
- moment_kv: float32 [1024, 2048], P(('shard', 'section'), 'tensor'), may hold values from -0.1 to 0.1
- moment_gate: float32 [512, 2048], P(('shard', 'section'), 'tensor'), may hold values from -0.1 to 0.1
- moment_laurel: float32 [128, 2048], P(('shard', 'section'), 'tensor'), may hold values from -0.1 to 0.1
- second_kv: float32 [1024, 2048], P(('shard', 'section'), 'tensor'), may hold values from 0.01 to 1
- second_gate: float32 [512, 2048], P(('shard', 'section'), 'tensor'), may hold values from 0.01 to 1
- second_laurel: float32 [128, 2048], P(('shard', 'section'), 'tensor'), may hold values from 0.01 to 1
Outputs:
- new_master_kv: float32 [1024, 2048], P(('shard', 'section'), 'tensor')
- new_master_gate: float32 [512, 2048], P(('shard', 'section'), 'tensor')
- new_master_laurel: float32 [128, 2048], P(('shard', 'section'), 'tensor')
- new_moment_kv: float32 [1024, 2048], P(('shard', 'section'), 'tensor')
- new_moment_gate: float32 [512, 2048], P(('shard', 'section'), 'tensor')
- new_moment_laurel: float32 [128, 2048], P(('shard', 'section'), 'tensor')
- new_second_kv: float32 [1024, 2048], P(('shard', 'section'), 'tensor')
- new_second_gate: float32 [512, 2048], P(('shard', 'section'), 'tensor')
- new_second_laurel: float32 [128, 2048], P(('shard', 'section'), 'tensor')
- weights_kv: bfloat16 [1024, 2048], P(None, 'tensor')
- weights_gate: bfloat16 [512, 2048], P(None, 'tensor')
- weights_laurel: bfloat16 [128, 2048], P(None, 'tensor')
The draws below stay inside these ranges and needn't reach their ends.
All inputs are finite; a program needn't handle non-finite values.
Results may differ from the reference program's by a relative error of at most 0.015.
Values may be sent and summed in bfloat16 or wider, within the bound.
A program may use at most 64 MiB of HBM per device.

```python
import math
import jax
import jax.numpy as jnp
from jax import lax

D = 2048
KVW = 512
PLG = 256
RANK = 64
MB = 2
STEP = 10
REPL = 8


def gradient_draw(key, offset, row_count, plain_mix, target):
    key = jax.random.fold_in(key, offset)
    subkeys = jax.random.split(key, 6)
    copies = REPL * MB
    own_weight = plain_mix[0]
    shared_weight = plain_mix[1]
    own_part = jax.random.normal(subkeys[0], (copies, row_count, D), jnp.float32)
    shared_part = jax.random.normal(subkeys[5], (1, row_count, D), jnp.float32)
    sample = jnp.clip(own_weight * own_part + shared_weight * shared_part, -6.0, 6.0)
    spread = target / math.sqrt(own_weight * own_weight * copies + shared_weight * shared_weight * copies * copies)
    row_scale = jnp.exp(jax.random.uniform(subkeys[1], (row_count, 1), jnp.float32) * math.log(10.0))
    col_scale = jnp.exp(jax.random.uniform(subkeys[2], (1, D), jnp.float32) * math.log(10.0))
    row_rise = jnp.exp(jnp.arange(row_count, dtype=jnp.float32)[:, None] * (math.log(3.0) / row_count))
    col_rise = jnp.exp(jnp.arange(D, dtype=jnp.float32)[None, :] * (math.log(3.0) / D))
    owners = jax.random.permutation(subkeys[3], REPL)
    row_block = jnp.arange(row_count) // (row_count // REPL)
    replica = jnp.arange(copies) // MB
    boosted = 1.0 + 3.0 * (owners[replica][:, None] == row_block[None, :]).astype(jnp.float32)
    result = spread * sample * boosted[:, :, None] * row_scale * col_scale * row_rise * col_rise
    return result.astype(jnp.bfloat16)


def draw_grad_kv(key, part):
    return gradient_draw(key, 11, 2 * KVW, (1.0, 0.0), 1.0)


def draw_grad_gate(key, part):
    return gradient_draw(key, 23, 2 * PLG, (0.1, 1.0), 1.75)


def draw_grad_laurel(key, part):
    return gradient_draw(key, 37, 2 * RANK, (1.0, 0.25), 4.0)


def steps_of(key, dims, cuts, low, high):
    def one(dim, blocks):
        draws = jax.random.uniform(jax.random.fold_in(jax.random.fold_in(key, 6), dim), (blocks,), jnp.float32, low / len(cuts), high / len(cuts))
        return jnp.repeat(jnp.exp(draws), dims[dim] // blocks).reshape((-1,) + (1,) * (len(dims) - dim - 1))

    level = one(*cuts[0])
    for cut in cuts[1:]:
        level = level * one(*cut)
    return level


def setup_inputs(seed: int = 0) -> dict:
    key_of = jax.random.split(jax.random.key(seed), 13)
    return {
        "grad_kv": draw_grad_kv(jax.random.fold_in(key_of[12], 71), 0),
        "grad_gate": draw_grad_gate(jax.random.fold_in(key_of[12], 71), 0),
        "grad_laurel": draw_grad_laurel(jax.random.fold_in(key_of[12], 71), 0),
        "master_kv": jnp.clip(jax.random.uniform(key_of[3], (2 * KVW, D), jnp.float32, -0.1, 0.1) * steps_of(key_of[3], (2 * KVW, D), ((0, 8), (1, 4)), -0.4, 0.0), -0.1, 0.1),
        "master_gate": jnp.clip(jax.random.uniform(key_of[4], (2 * PLG, D), jnp.float32, -0.1, 0.1) * steps_of(key_of[4], (2 * PLG, D), ((0, 8), (1, 4)), -0.4, 0.0), -0.1, 0.1),
        "master_laurel": jnp.clip(jax.random.uniform(key_of[5], (2 * RANK, D), jnp.float32, -0.1, 0.1) * steps_of(key_of[5], (2 * RANK, D), ((0, 8), (1, 4)), -0.4, 0.0), -0.1, 0.1),
        "moment_kv": jnp.clip(jax.random.uniform(key_of[6], (2 * KVW, D), jnp.float32, -0.1, 0.1) * steps_of(key_of[6], (2 * KVW, D), ((0, 8), (1, 4)), -0.4, 0.0), -0.1, 0.1),
        "moment_gate": jnp.clip(jax.random.uniform(key_of[7], (2 * PLG, D), jnp.float32, -0.1, 0.1) * steps_of(key_of[7], (2 * PLG, D), ((0, 8), (1, 4)), -0.4, 0.0), -0.1, 0.1),
        "moment_laurel": jnp.clip(jax.random.uniform(key_of[8], (2 * RANK, D), jnp.float32, -0.1, 0.1) * steps_of(key_of[8], (2 * RANK, D), ((0, 8), (1, 4)), -0.4, 0.0), -0.1, 0.1),
        "second_kv": jnp.clip(jnp.exp(math.log(1.0) - 4.6051702 * jax.random.uniform(key_of[9], (2 * KVW, D), jnp.float32) ** steps_of(key_of[9], (2 * KVW, D), ((0, 8), (1, 4)), -0.2, 0.2)), 0.01, 1.0),
        "second_gate": jnp.clip(jnp.exp(math.log(1.0) - 4.6051702 * jax.random.uniform(key_of[10], (2 * PLG, D), jnp.float32) ** steps_of(key_of[10], (2 * PLG, D), ((0, 8), (1, 4)), -0.2, 0.2)), 0.01, 1.0),
        "second_laurel": jnp.clip(jnp.exp(math.log(1.0) - 4.6051702 * jax.random.uniform(key_of[11], (2 * RANK, D), jnp.float32) ** steps_of(key_of[11], (2 * RANK, D), ((0, 8), (1, 4)), -0.2, 0.2)), 0.01, 1.0),
    }


beta_one = 0.9
beta_two = 0.95
adam_eps = 1e-08
learn_rate = 0.05
weight_decay = 0.1
clip_rms = 0.5

def adamw_group(master, moment, second, summed, factor):
    clipped = factor * summed
    moment_new = beta_one * moment + (1.0 - beta_one) * clipped
    second_new = beta_two * second + (1.0 - beta_two) * clipped * clipped
    first_hat = moment_new / (1.0 - beta_one ** STEP)
    second_hat = second_new / (1.0 - beta_two ** STEP)
    master_new = master - learn_rate * (first_hat / (jnp.sqrt(second_hat) + adam_eps) + weight_decay * master)
    return (master_new, moment_new, second_new)

def reference(grad_kv, grad_gate, grad_laurel, master_kv, master_gate, master_laurel, moment_kv, moment_gate, moment_laurel, second_kv, second_gate, second_laurel):
    sums_all = [lax.optimization_barrier(jnp.sum(gradient, axis=0, dtype=jnp.float32)) for gradient in (grad_kv, grad_gate, grad_laurel)]
    squares = jnp.sum(sums_all[0] * sums_all[0]) + jnp.sum(sums_all[1] * sums_all[1]) + jnp.sum(sums_all[2] * sums_all[2])
    entries = sums_all[0].size + sums_all[1].size + sums_all[2].size
    ceiling = clip_rms * math.sqrt(entries)
    factor = ceiling / jnp.maximum(jnp.sqrt(squares), ceiling)
    kv_out = adamw_group(master_kv, moment_kv, second_kv, sums_all[0], factor)
    gate_out = adamw_group(master_gate, moment_gate, second_gate, sums_all[1], factor)
    laurel_out = adamw_group(master_laurel, moment_laurel, second_laurel, sums_all[2], factor)
    return (kv_out[0], gate_out[0], laurel_out[0], kv_out[1], gate_out[1], laurel_out[1], kv_out[2], gate_out[2], laurel_out[2], kv_out[0].astype(jnp.bfloat16), gate_out[0].astype(jnp.bfloat16), laurel_out[0].astype(jnp.bfloat16))
```

```python
import functools
import math

import jax
import jax.numpy as jnp
from jax import lax
from jax.experimental import pallas as pl
from jax.experimental.pallas import tpu as pltpu
from jax.sharding import PartitionSpec as P

STEP = 10

beta_one = 0.9
beta_two = 0.95
adam_eps = 1e-08
learn_rate = 0.05
weight_decay = 0.1
clip_rms = 0.5

WIRE = jnp.bfloat16
MESH = pl.DeviceIdType.MESH


def adamw_group(master, moment, second, summed, factor):
    clipped = factor * summed
    moment_new = beta_one * moment + (1.0 - beta_one) * clipped
    second_new = beta_two * second + (1.0 - beta_two) * clipped * clipped
    first_hat = moment_new / (1.0 - beta_one**STEP)
    second_hat = second_new / (1.0 - beta_two**STEP)
    master_new = master - learn_rate * (
        first_hat / (jnp.sqrt(second_hat) + adam_eps) + weight_decay * master
    )
    return (master_new, moment_new, second_new)


def section_order(count):
    return sorted(range(1, count), key=lambda k: (abs(k - count // 2), -k)) + [0]


def kernel(sizes, rows, batches, ceiling, *refs):
    shards, sections, tensors = sizes
    grads, states = refs[0:3], refs[3:12]
    new_states, weights = refs[12:21], refs[21]
    grad_buf, state_buf, new_buf = refs[22:25], refs[25:34], refs[34:43]
    (
        x_out, x_in, z_out, z_in, total, own_weights,
        norm_out, group_in, tensor_out, tensor_in,
        load_sem, state_sem, store_sem, own_sem,
        x_send, x_recv, z_send, z_recv,
        group_send, group_recv, tensor_send, tensor_recv,
        gz_send, gz_recv, gx_send, gx_recv,
    ) = refs[43:]
    s, t, z = lax.axis_index("shard"), lax.axis_index("tensor"), lax.axis_index("section")
    order = section_order(sections)
    starts = [sum(rows[:g]) for g in range(3)]

    def shard_at(j):
        return lax.rem(s + j, shards)

    def section_at(k):
        return lax.rem(z + k, sections)

    group = [(a, b) for a in range(shards) for b in range(sections) if (a, b) != (0, 0)]

    barrier = pltpu.get_barrier_semaphore()
    for a, b in group:
        pl.semaphore_signal(
            barrier, inc=1, device_id={"shard": shard_at(a), "section": section_at(b)}, device_id_type=MESH
        )
    for c in range(1, tensors):
        pl.semaphore_signal(barrier, inc=1, device_id={"tensor": lax.rem(t + c, tensors)}, device_id_type=MESH)

    loads = {}
    for j in list(range(1, shards)) + [0]:
        for g in range(3):
            copy = pltpu.make_async_copy(
                grads[g].at[:, shard_at(j)], grad_buf[g].at[:, shard_at(j)], load_sem.at[j, g]
            )
            copy.start()
            loads[j, g] = copy
    state_loads = []
    for i in range(9):
        copy = pltpu.make_async_copy(states[i], state_buf[i], state_sem.at[i])
        copy.start()
        state_loads.append(copy)

    def partial(g, shard, section):
        value = grad_buf[g][0, shard, section].astype(jnp.float32)
        for m in range(1, batches):
            value = value + grad_buf[g][m, shard, section].astype(jnp.float32)
        return value

    sends = []
    x_copies = {}
    waited = set()
    for k in order:
        for j in range(1, shards):
            for g in range(3):
                if (j, g) not in waited:
                    loads[j, g].wait()
                    waited.add((j, g))
                x_out[j - 1, k, starts[g] : starts[g] + rows[g]] = partial(
                    g, shard_at(j), section_at(k)
                ).astype(WIRE)
        if k == order[0]:
            pl.semaphore_wait(barrier, len(group) + tensors - 1)
        for j in range(1, shards):
            copy = pltpu.make_async_remote_copy(
                src_ref=x_out.at[j - 1, k],
                dst_ref=x_in.at[j - 1, k],
                send_sem=x_send.at[j - 1, k],
                recv_sem=x_recv.at[j - 1, k],
                device_id={"shard": shard_at(j)},
                device_id_type=MESH,
            )
            copy.start()
            x_copies[j, k] = copy
            sends.append(copy)

    for g in range(3):
        loads[0, g].wait()
    z_copies = {}
    for k in order:
        for j in range(1, shards):
            x_copies[j, k].wait_recv()
        for g in range(3):
            span = slice(starts[g], starts[g] + rows[g])
            value = partial(g, s, section_at(k))
            for j in range(1, shards):
                value = value + x_in[j - 1, k, span].astype(jnp.float32)
            if k:
                z_out[k - 1, span] = value.astype(WIRE)
            else:
                total[span] = value
        if k:
            copy = pltpu.make_async_remote_copy(
                src_ref=z_out.at[k - 1],
                dst_ref=z_in.at[k - 1],
                send_sem=z_send.at[k - 1],
                recv_sem=z_recv.at[k - 1],
                device_id={"section": section_at(k)},
                device_id_type=MESH,
            )
            copy.start()
            z_copies[k] = copy
            sends.append(copy)
    for k in order[:-1]:
        z_copies[k].wait_recv()
    summed = total[...]
    for k in order[:-1]:
        summed = summed + z_in[k - 1].astype(jnp.float32)
    total[...] = summed

    def fold(value):
        width = value.shape[1]
        return sum(value[:, c : c + 128] for c in range(0, width, 128))

    squares = fold(jnp.sum(summed * summed, axis=0, keepdims=True))
    norm_out[...] = jnp.broadcast_to(squares, norm_out.shape)
    group_copies = []
    for i, (a, b) in enumerate(group):
        copy = pltpu.make_async_remote_copy(
            src_ref=norm_out,
            dst_ref=group_in.at[i],
            send_sem=group_send.at[i],
            recv_sem=group_recv.at[i],
            device_id={"shard": shard_at(a), "section": section_at(b)},
            device_id_type=MESH,
        )
        copy.start()
        group_copies.append(copy)
        sends.append(copy)
    for copy in state_loads:
        copy.wait()
    value = norm_out[...]
    for i, copy in enumerate(group_copies):
        copy.wait_recv()
        value = value + group_in[i]
    tensor_out[...] = value
    tensor_copies = []
    for c in range(1, tensors):
        copy = pltpu.make_async_remote_copy(
            src_ref=tensor_out,
            dst_ref=tensor_in.at[c - 1],
            send_sem=tensor_send.at[c - 1],
            recv_sem=tensor_recv.at[c - 1],
            device_id={"tensor": lax.rem(t + c, tensors)},
            device_id_type=MESH,
        )
        copy.start()
        tensor_copies.append(copy)
        sends.append(copy)
    for i, copy in enumerate(tensor_copies):
        copy.wait_recv()
        value = value + tensor_in[i]
    norm = jnp.sqrt(jnp.sum(value[0:1], axis=1, keepdims=True))
    factor = ceiling / jnp.maximum(norm, ceiling)

    for g in range(3):
        span = slice(starts[g], starts[g] + rows[g])
        new = adamw_group(
            state_buf[g][...], state_buf[3 + g][...], state_buf[6 + g][...], total[span], factor
        )
        own_weights[span] = new[0].astype(jnp.bfloat16)
        for i in range(3):
            new_buf[3 * i + g][...] = new[i]

    gx_copies = {}

    def forward(k, source):
        for j in range(1, shards):
            copy = pltpu.make_async_remote_copy(
                src_ref=source,
                dst_ref=weights.at[s, lax.rem(z - k + sections, sections)],
                send_sem=gx_send.at[j - 1, k],
                recv_sem=gx_recv.at[j - 1, k],
                device_id={"shard": shard_at(j)},
                device_id_type=MESH,
            )
            copy.start()
            gx_copies[j, k] = copy
            sends.append(copy)

    forward(0, own_weights)
    gz_copies = {}
    for k in order[:-1]:
        copy = pltpu.make_async_remote_copy(
            src_ref=own_weights,
            dst_ref=weights.at[s, z],
            send_sem=gz_send.at[k - 1],
            recv_sem=gz_recv.at[k - 1],
            device_id={"section": section_at(k)},
            device_id_type=MESH,
        )
        copy.start()
        gz_copies[k] = copy
        sends.append(copy)
    own = pltpu.make_async_copy(own_weights, weights.at[s, z], own_sem)
    own.start()
    stores = []
    for i in range(9):
        copy = pltpu.make_async_copy(new_buf[i], new_states[i], store_sem.at[i])
        copy.start()
        stores.append(copy)
    for k in reversed(order[:-1]):
        gz_copies[k].wait_recv()
        forward(k, weights.at[s, lax.rem(z - k + sections, sections)])
    own.wait()
    for copy in stores:
        copy.wait()
    for copy in gx_copies.values():
        copy.wait_recv()
    for copy in sends:
        copy.wait_send()


def on_device(*arguments):
    shards, sections, tensors = (lax.axis_size(a) for a in ("shard", "section", "tensor"))
    grads, states = arguments[:3], arguments[3:]
    batches, _, width = grads[0].shape
    rows = [states[g].shape[0] for g in range(3)]
    height = sum(rows)
    entries = sum(gradient.shape[1] * width * tensors for gradient in grads)
    ceiling = clip_rms * math.sqrt(entries)
    grads = [
        gradient.reshape(batches, shards, sections, rows[g], width) for g, gradient in enumerate(grads)
    ]
    n_group = shards * sections - 1
    dma = pltpu.SemaphoreType.DMA
    scratch = (
        [pltpu.VMEM(gradient.shape, jnp.bfloat16) for gradient in grads]
        + [pltpu.VMEM(state.shape, jnp.float32) for state in states]
        + [pltpu.VMEM(state.shape, jnp.float32) for state in states]
        + [
            pltpu.VMEM((shards - 1, sections, height, width), WIRE),
            pltpu.VMEM((shards - 1, sections, height, width), WIRE),
            pltpu.VMEM((sections - 1, height, width), WIRE),
            pltpu.VMEM((sections - 1, height, width), WIRE),
            pltpu.VMEM((height, width), jnp.float32),
            pltpu.VMEM((height, width), jnp.bfloat16),
            pltpu.VMEM((8, 128), jnp.float32),
            pltpu.VMEM((n_group, 8, 128), jnp.float32),
            pltpu.VMEM((8, 128), jnp.float32),
            pltpu.VMEM((tensors - 1, 8, 128), jnp.float32),
            dma((shards, 3)),
            dma((9,)),
            dma((9,)),
            dma,
            dma((shards - 1, sections)),
            dma((shards - 1, sections)),
            dma((sections - 1,)),
            dma((sections - 1,)),
            dma((n_group,)),
            dma((n_group,)),
            dma((tensors - 1,)),
            dma((tensors - 1,)),
            dma((sections - 1,)),
            dma((sections - 1,)),
            dma((shards - 1, sections)),
            dma((shards - 1, sections)),
        ]
    )
    results = pl.pallas_call(
        functools.partial(kernel, (shards, sections, tensors), rows, batches, ceiling),
        out_shape=[jax.ShapeDtypeStruct(state.shape, jnp.float32) for state in states]
        + [jax.ShapeDtypeStruct((shards, sections, height, width), jnp.bfloat16)],
        in_specs=[pl.BlockSpec(memory_space=pl.ANY)] * 12,
        out_specs=[pl.BlockSpec(memory_space=pl.ANY)] * 10,
        scratch_shapes=scratch,
        compiler_params=pltpu.CompilerParams(
            collective_id=0, has_side_effects=True, vmem_limit_bytes=48 * 1024 * 1024
        ),
    )(*grads, *states)
    weights = []
    for g in range(3):
        start = sum(rows[:g])
        part = lax.slice_in_dim(results[9], start, start + rows[g], axis=2)
        weights.append(part.reshape(shards * sections * rows[g], width))
    return (*results[:9], *weights)


def solution(mesh):
    grad = P(("shard", "section"), None, "tensor")
    state = P(("shard", "section"), "tensor")
    return jax.shard_map(
        on_device,
        mesh=mesh,
        in_specs=(grad,) * 3 + (state,) * 9,
        out_specs=(state,) * 9 + (P(None, "tensor"),) * 3,
        check_vma=False,
    )
```

```python
import functools
import math

import jax
import jax.numpy as jnp
from jax import lax
from jax.experimental import pallas as pl
from jax.experimental.pallas import tpu as pltpu
from jax.sharding import PartitionSpec as P

STEP = 10

beta_one = 0.9
beta_two = 0.95
adam_eps = 1e-08
learn_rate = 0.05
weight_decay = 0.1
clip_rms = 0.5

WIRE = jnp.bfloat16
VMEM_LIMIT = 56 * 1024 * 1024
MESH = pl.DeviceIdType.MESH


def adamw_group(master, moment, second, summed, factor):
    clipped = factor * summed
    moment_new = beta_one * moment + (1.0 - beta_one) * clipped
    second_new = beta_two * second + (1.0 - beta_two) * clipped * clipped
    first_hat = moment_new / (1.0 - beta_one**STEP)
    second_hat = second_new / (1.0 - beta_two**STEP)
    master_new = master - learn_rate * (
        first_hat / (jnp.sqrt(second_hat) + adam_eps) + weight_decay * master
    )
    return (master_new, moment_new, second_new)


def section_order(count):
    return sorted(range(1, count), key=lambda k: (abs(k - count // 2), -k)) + [0]


def kernel(sizes, rows, batches, ceiling, *refs):
    shards, sections, tensors = sizes
    grads, states = refs[0:3], refs[3:12]
    new_states, weights = refs[12:21], refs[21]
    grad_buf, state_buf, new_buf = refs[22:25], refs[25:34], refs[34:43]
    (
        x_out, x_in, z_out, z_in, total, own_weights,
        norm_out, group_in, tensor_out, tensor_in,
        load_sem, state_sem, store_sem, own_sem,
        x_send, x_recv, z_send, z_recv,
        group_send, group_recv, tensor_send, tensor_recv,
        gz_send, gz_recv, gx_send, gx_recv,
    ) = refs[43:]
    s, t, z = lax.axis_index("shard"), lax.axis_index("tensor"), lax.axis_index("section")
    order = section_order(sections)
    starts = [sum(rows[:g]) for g in range(3)]

    def shard_at(j):
        return lax.rem(s + j, shards)

    def section_at(k):
        return lax.rem(z + k, sections)

    group = [(a, b) for a in range(shards) for b in range(sections) if (a, b) != (0, 0)]

    barrier = pltpu.get_barrier_semaphore()
    for a, b in group:
        pl.semaphore_signal(
            barrier, inc=1, device_id={"shard": shard_at(a), "section": section_at(b)}, device_id_type=MESH
        )
    for c in range(1, tensors):
        pl.semaphore_signal(barrier, inc=1, device_id={"tensor": lax.rem(t + c, tensors)}, device_id_type=MESH)

    loads = {}
    for j in list(range(1, shards)) + [0]:
        for g in range(3):
            copy = pltpu.make_async_copy(
                grads[g].at[:, shard_at(j)], grad_buf[g].at[:, shard_at(j)], load_sem.at[j, g]
            )
            copy.start()
            loads[j, g] = copy
    state_loads = []
    for i in range(9):
        copy = pltpu.make_async_copy(states[i], state_buf[i], state_sem.at[i])
        copy.start()
        state_loads.append(copy)

    def partial(g, shard, section):
        value = grad_buf[g][0, shard, section].astype(jnp.float32)
        for m in range(1, batches):
            value = value + grad_buf[g][m, shard, section].astype(jnp.float32)
        return value

    sends = []
    x_copies = {}
    waited = set()
    for k in order:
        for j in range(1, shards):
            for g in range(3):
                if (j, g) not in waited:
                    loads[j, g].wait()
                    waited.add((j, g))
                x_out[j - 1, k, starts[g] : starts[g] + rows[g]] = partial(
                    g, shard_at(j), section_at(k)
                ).astype(WIRE)
        if k == order[0]:
            pl.semaphore_wait(barrier, len(group) + tensors - 1)
        for j in range(1, shards):
            copy = pltpu.make_async_remote_copy(
                src_ref=x_out.at[j - 1, k],
                dst_ref=x_in.at[j - 1, k],
                send_sem=x_send.at[j - 1, k],
                recv_sem=x_recv.at[j - 1, k],
                device_id={"shard": shard_at(j)},
                device_id_type=MESH,
            )
            copy.start()
            x_copies[j, k] = copy
            sends.append(copy)

    for g in range(3):
        loads[0, g].wait()
    z_copies = {}
    for k in order:
        for j in range(1, shards):
            x_copies[j, k].wait_recv()
        for g in range(3):
            span = slice(starts[g], starts[g] + rows[g])
            value = partial(g, s, section_at(k))
            for j in range(1, shards):
                value = value + x_in[j - 1, k, span].astype(jnp.float32)
            if k:
                z_out[k - 1, span] = value.astype(WIRE)
            else:
                total[span] = value
        if k:
            copy = pltpu.make_async_remote_copy(
                src_ref=z_out.at[k - 1],
                dst_ref=z_in.at[k - 1],
                send_sem=z_send.at[k - 1],
                recv_sem=z_recv.at[k - 1],
                device_id={"section": section_at(k)},
                device_id_type=MESH,
            )
            copy.start()
            z_copies[k] = copy
            sends.append(copy)
    for k in order[:-1]:
        z_copies[k].wait_recv()
    summed = total[...]
    for k in order[:-1]:
        summed = summed + z_in[k - 1].astype(jnp.float32)
    total[...] = summed

    def fold(value):
        width = value.shape[1]
        return sum(value[:, c : c + 128] for c in range(0, width, 128))

    squares = fold(jnp.sum(summed * summed, axis=0, keepdims=True))
    norm_out[...] = jnp.broadcast_to(squares, norm_out.shape)
    group_copies = []
    for i, (a, b) in enumerate(group):
        copy = pltpu.make_async_remote_copy(
            src_ref=norm_out,
            dst_ref=group_in.at[i],
            send_sem=group_send.at[i],
            recv_sem=group_recv.at[i],
            device_id={"shard": shard_at(a), "section": section_at(b)},
            device_id_type=MESH,
        )
        copy.start()
        group_copies.append(copy)
        sends.append(copy)
    for copy in state_loads:
        copy.wait()
    value = norm_out[...]
    for i, copy in enumerate(group_copies):
        copy.wait_recv()
        value = value + group_in[i]
    tensor_out[...] = value
    tensor_copies = []
    for c in range(1, tensors):
        copy = pltpu.make_async_remote_copy(
            src_ref=tensor_out,
            dst_ref=tensor_in.at[c - 1],
            send_sem=tensor_send.at[c - 1],
            recv_sem=tensor_recv.at[c - 1],
            device_id={"tensor": lax.rem(t + c, tensors)},
            device_id_type=MESH,
        )
        copy.start()
        tensor_copies.append(copy)
        sends.append(copy)
    for i, copy in enumerate(tensor_copies):
        copy.wait_recv()
        value = value + tensor_in[i]
    norm = jnp.sqrt(jnp.sum(value[0:1], axis=1, keepdims=True))
    factor = ceiling / jnp.maximum(norm, ceiling)

    for g in range(3):
        span = slice(starts[g], starts[g] + rows[g])
        new = adamw_group(
            state_buf[g][...], state_buf[3 + g][...], state_buf[6 + g][...], total[span], factor
        )
        own_weights[span] = new[0].astype(jnp.bfloat16)
        for i in range(3):
            new_buf[3 * i + g][...] = new[i]

    gx_copies = {}

    def forward(k, source):
        for j in range(1, shards):
            copy = pltpu.make_async_remote_copy(
                src_ref=source,
                dst_ref=weights.at[s, lax.rem(z - k + sections, sections)],
                send_sem=gx_send.at[j - 1, k],
                recv_sem=gx_recv.at[j - 1, k],
                device_id={"shard": shard_at(j)},
                device_id_type=MESH,
            )
            copy.start()
            gx_copies[j, k] = copy
            sends.append(copy)

    forward(0, own_weights)
    gz_copies = {}
    for k in order[:-1]:
        copy = pltpu.make_async_remote_copy(
            src_ref=own_weights,
            dst_ref=weights.at[s, z],
            send_sem=gz_send.at[k - 1],
            recv_sem=gz_recv.at[k - 1],
            device_id={"section": section_at(k)},
            device_id_type=MESH,
        )
        copy.start()
        gz_copies[k] = copy
        sends.append(copy)
    own = pltpu.make_async_copy(own_weights, weights.at[s, z], own_sem)
    own.start()
    stores = []
    for i in range(9):
        copy = pltpu.make_async_copy(new_buf[i], new_states[i], store_sem.at[i])
        copy.start()
        stores.append(copy)
    for k in reversed(order[:-1]):
        gz_copies[k].wait_recv()
        forward(k, weights.at[s, lax.rem(z - k + sections, sections)])
    own.wait()
    for copy in stores:
        copy.wait()
    for copy in gx_copies.values():
        copy.wait_recv()
    for copy in sends:
        copy.wait_send()


def finish(rows, *refs):
    sources, targets, sem = refs[:10], refs[10:22], refs[22]
    copies = []
    for g in range(3):
        start = sum(rows[:g])
        copies.append((sources[9].at[:, :, start : start + rows[g]], targets[9 + g]))
    copies += list(zip(sources[:9], targets[:9]))
    copies = [
        pltpu.make_async_copy(source, target, sem.at[i]) for i, (source, target) in enumerate(copies)
    ]
    for copy in copies:
        copy.start()
    for copy in copies:
        copy.wait()


def on_device(*arguments):
    shards, sections, tensors = (lax.axis_size(a) for a in ("shard", "section", "tensor"))
    grads, states = arguments[:3], arguments[3:]
    batches, _, width = grads[0].shape
    rows = [states[g].shape[0] for g in range(3)]
    height = sum(rows)
    entries = sum(gradient.shape[1] * width * tensors for gradient in grads)
    ceiling = clip_rms * math.sqrt(entries)
    grads = [
        gradient.reshape(batches, shards, sections, rows[g], width) for g, gradient in enumerate(grads)
    ]
    n_group = shards * sections - 1
    dma = pltpu.SemaphoreType.DMA
    scratch = (
        [pltpu.VMEM(gradient.shape, jnp.bfloat16) for gradient in grads]
        + [pltpu.VMEM(state.shape, jnp.float32) for state in states]
        + [pltpu.VMEM(state.shape, jnp.float32) for state in states]
        + [
            pltpu.VMEM((shards - 1, sections, height, width), WIRE),
            pltpu.VMEM((shards - 1, sections, height, width), WIRE),
            pltpu.VMEM((sections - 1, height, width), WIRE),
            pltpu.VMEM((sections - 1, height, width), WIRE),
            pltpu.VMEM((height, width), jnp.float32),
            pltpu.VMEM((height, width), jnp.bfloat16),
            pltpu.VMEM((8, 128), jnp.float32),
            pltpu.VMEM((n_group, 8, 128), jnp.float32),
            pltpu.VMEM((8, 128), jnp.float32),
            pltpu.VMEM((tensors - 1, 8, 128), jnp.float32),
            dma((shards, 3)),
            dma((9,)),
            dma((9,)),
            dma,
            dma((shards - 1, sections)),
            dma((shards - 1, sections)),
            dma((sections - 1,)),
            dma((sections - 1,)),
            dma((n_group,)),
            dma((n_group,)),
            dma((tensors - 1,)),
            dma((tensors - 1,)),
            dma((sections - 1,)),
            dma((sections - 1,)),
            dma((shards - 1, sections)),
            dma((shards - 1, sections)),
        ]
    )
    results = pl.pallas_call(
        functools.partial(kernel, (shards, sections, tensors), rows, batches, ceiling),
        out_shape=[pltpu.VMEM(state.shape, jnp.float32) for state in states]
        + [pltpu.VMEM((shards, sections, height, width), jnp.bfloat16)],
        in_specs=[pl.BlockSpec(memory_space=pltpu.HBM)] * 12,
        out_specs=[pl.BlockSpec(memory_space=pltpu.VMEM)] * 10,
        scratch_shapes=scratch,
        compiler_params=pltpu.CompilerParams(
            collective_id=0, has_side_effects=True, vmem_limit_bytes=VMEM_LIMIT
        ),
    )(*grads, *states)
    full = [
        jax.ShapeDtypeStruct((shards, sections, rows[g], width), jnp.bfloat16) for g in range(3)
    ]
    finished = pl.pallas_call(
        functools.partial(finish, rows),
        out_shape=[jax.ShapeDtypeStruct(state.shape, jnp.float32) for state in states] + full,
        in_specs=[pl.BlockSpec(memory_space=pl.ANY)] * 10,
        out_specs=[pl.BlockSpec(memory_space=pltpu.HBM)] * 12,
        scratch_shapes=[dma((12,))],
        compiler_params=pltpu.CompilerParams(vmem_limit_bytes=4 * 1024 * 1024),
    )(*results)
    weights = [part.reshape(-1, width) for part in finished[9:]]
    return (*finished[:9], *weights)


def solution(mesh):
    grad = P(("shard", "section"), None, "tensor")
    state = P(("shard", "section"), "tensor")
    return jax.shard_map(
        on_device,
        mesh=mesh,
        in_specs=(grad,) * 3 + (state,) * 9,
        out_specs=(state,) * 9 + (P(None, "tensor"),) * 3,
        check_vma=False,
    )
```

```python
import functools
import math

import jax
import jax.numpy as jnp
from jax import lax
from jax.experimental import pallas as pl
from jax.experimental.pallas import tpu as pltpu
from jax.sharding import PartitionSpec as P

STEP = 10

beta_one = 0.9
beta_two = 0.95
adam_eps = 1e-08
learn_rate = 0.05
weight_decay = 0.1
clip_rms = 0.5

WIRE = jnp.bfloat16
VMEM_LIMIT = 56 * 1024 * 1024
PIECES = 4
DEPTH = 2
MESH = pl.DeviceIdType.MESH


def adamw_group(master, moment, second, summed, factor):
    clipped = factor * summed
    moment_new = beta_one * moment + (1.0 - beta_one) * clipped
    second_new = beta_two * second + (1.0 - beta_two) * clipped * clipped
    first_hat = moment_new / (1.0 - beta_one**STEP)
    second_hat = second_new / (1.0 - beta_two**STEP)
    master_new = master - learn_rate * (
        first_hat / (jnp.sqrt(second_hat) + adam_eps) + weight_decay * master
    )
    return (master_new, moment_new, second_new)


def section_order(count):
    return sorted(range(1, count), key=lambda k: (abs(k - count // 2), -k)) + [0]


def kernel(sizes, rows, batches, ceiling, *refs):
    shards, sections, tensors = sizes
    grads, states = refs[0:3], refs[3:12]
    new_states, weights = refs[12:21], refs[21]
    grad_buf, state_buf, new_buf = refs[22:25], refs[25:34], refs[34:43]
    (
        x_out, x_in, z_out, z_in, total, own_weights,
        norm_out, group_in, tensor_out, tensor_in,
        load_sem, state_sem, store_sem, own_sem,
        x_send, x_recv, z_send, z_recv,
        group_send, group_recv, tensor_send, tensor_recv,
        gz_send, gz_recv, gx_send, gx_recv,
    ) = refs[43:]
    s, t, z = lax.axis_index("shard"), lax.axis_index("tensor"), lax.axis_index("section")
    order = section_order(sections)
    starts = [sum(rows[:g]) for g in range(3)]

    def shard_at(j):
        return lax.rem(s + j, shards)

    def section_at(k):
        return lax.rem(z + k, sections)

    group = [(a, b) for a in range(shards) for b in range(sections) if (a, b) != (0, 0)]

    barrier = pltpu.get_barrier_semaphore()
    for a, b in group:
        pl.semaphore_signal(
            barrier, inc=1, device_id={"shard": shard_at(a), "section": section_at(b)}, device_id_type=MESH
        )
    for c in range(1, tensors):
        pl.semaphore_signal(barrier, inc=1, device_id={"tensor": lax.rem(t + c, tensors)}, device_id_type=MESH)

    loads = {}
    for j in list(range(1, shards)) + [0]:
        for g in range(3):
            copy = pltpu.make_async_copy(
                grads[g].at[:, shard_at(j)], grad_buf[g].at[:, shard_at(j)], load_sem.at[j, g]
            )
            copy.start()
            loads[j, g] = copy
    state_loads = []
    for i in range(9):
        copy = pltpu.make_async_copy(states[i], state_buf[i], state_sem.at[i])
        copy.start()
        state_loads.append(copy)

    def partial(g, shard, section):
        value = grad_buf[g][0, shard, section].astype(jnp.float32)
        for m in range(1, batches):
            value = value + grad_buf[g][m, shard, section].astype(jnp.float32)
        return value

    sends = []
    x_copies = {}
    waited = set()
    for k in order:
        for j in range(1, shards):
            for g in range(3):
                if (j, g) not in waited:
                    loads[j, g].wait()
                    waited.add((j, g))
                x_out[j - 1, k, starts[g] : starts[g] + rows[g]] = partial(
                    g, shard_at(j), section_at(k)
                ).astype(WIRE)
        if k == order[0]:
            pl.semaphore_wait(barrier, len(group) + tensors - 1)
        for j in range(1, shards):
            copy = pltpu.make_async_remote_copy(
                src_ref=x_out.at[j - 1, k],
                dst_ref=x_in.at[j - 1, k],
                send_sem=x_send.at[j - 1, k],
                recv_sem=x_recv.at[j - 1, k],
                device_id={"shard": shard_at(j)},
                device_id_type=MESH,
            )
            copy.start()
            x_copies[j, k] = copy
            sends.append(copy)

    for g in range(3):
        loads[0, g].wait()
    z_copies = {}
    for k in order:
        for j in range(1, shards):
            x_copies[j, k].wait_recv()
        for g in range(3):
            span = slice(starts[g], starts[g] + rows[g])
            value = partial(g, s, section_at(k))
            for j in range(1, shards):
                value = value + x_in[j - 1, k, span].astype(jnp.float32)
            if k:
                z_out[k - 1, span] = value.astype(WIRE)
            else:
                total[span] = value
        if k:
            copy = pltpu.make_async_remote_copy(
                src_ref=z_out.at[k - 1],
                dst_ref=z_in.at[k - 1],
                send_sem=z_send.at[k - 1],
                recv_sem=z_recv.at[k - 1],
                device_id={"section": section_at(k)},
                device_id_type=MESH,
            )
            copy.start()
            z_copies[k] = copy
            sends.append(copy)
    for k in order[:-1]:
        z_copies[k].wait_recv()
    summed = total[...]
    for k in order[:-1]:
        summed = summed + z_in[k - 1].astype(jnp.float32)
    total[...] = summed

    def fold(value):
        width = value.shape[1]
        return sum(value[:, c : c + 128] for c in range(0, width, 128))

    squares = fold(jnp.sum(summed * summed, axis=0, keepdims=True))
    norm_out[...] = jnp.broadcast_to(squares, norm_out.shape)
    group_copies = []
    for i, (a, b) in enumerate(group):
        copy = pltpu.make_async_remote_copy(
            src_ref=norm_out,
            dst_ref=group_in.at[i],
            send_sem=group_send.at[i],
            recv_sem=group_recv.at[i],
            device_id={"shard": shard_at(a), "section": section_at(b)},
            device_id_type=MESH,
        )
        copy.start()
        group_copies.append(copy)
        sends.append(copy)
    for copy in state_loads:
        copy.wait()
    value = norm_out[...]
    for i, copy in enumerate(group_copies):
        copy.wait_recv()
        value = value + group_in[i]
    tensor_out[...] = value
    tensor_copies = []
    for c in range(1, tensors):
        copy = pltpu.make_async_remote_copy(
            src_ref=tensor_out,
            dst_ref=tensor_in.at[c - 1],
            send_sem=tensor_send.at[c - 1],
            recv_sem=tensor_recv.at[c - 1],
            device_id={"tensor": lax.rem(t + c, tensors)},
            device_id_type=MESH,
        )
        copy.start()
        tensor_copies.append(copy)
        sends.append(copy)
    for i, copy in enumerate(tensor_copies):
        copy.wait_recv()
        value = value + tensor_in[i]
    norm = jnp.sqrt(jnp.sum(value[0:1], axis=1, keepdims=True))
    factor = ceiling / jnp.maximum(norm, ceiling)

    for g in range(3):
        span = slice(starts[g], starts[g] + rows[g])
        new = adamw_group(
            state_buf[g][...], state_buf[3 + g][...], state_buf[6 + g][...], total[span], factor
        )
        own_weights[span] = new[0].astype(jnp.bfloat16)
        for i in range(3):
            new_buf[3 * i + g][...] = new[i]

    width = own_weights.shape[1] // PIECES
    gx_copies = {}
    gz_copies = {}

    def piece(ref, c):
        return ref.at[:, c * width : (c + 1) * width]

    def forward(k, c):
        place = weights.at[s, lax.rem(z - k + sections, sections)]
        for j in range(1, shards):
            copy = pltpu.make_async_remote_copy(
                src_ref=piece(place if k else own_weights, c),
                dst_ref=piece(place, c),
                send_sem=gx_send.at[j - 1, k, c],
                recv_sem=gx_recv.at[j - 1, k, c],
                device_id={"shard": shard_at(j)},
                device_id_type=MESH,
            )
            copy.start()
            gx_copies[j, k, c] = copy
            sends.append(copy)

    def spread(c):
        for k in order[:-1]:
            copy = pltpu.make_async_remote_copy(
                src_ref=piece(own_weights, c),
                dst_ref=piece(weights.at[s, z], c),
                send_sem=gz_send.at[k - 1, c],
                recv_sem=gz_recv.at[k - 1, c],
                device_id={"section": section_at(k)},
                device_id_type=MESH,
            )
            copy.start()
            gz_copies[k, c] = copy
            sends.append(copy)
        forward(0, c)

    for c in range(min(DEPTH, PIECES)):
        spread(c)
    own = pltpu.make_async_copy(own_weights, weights.at[s, z], own_sem)
    own.start()
    stores = []
    for i in range(9):
        copy = pltpu.make_async_copy(new_buf[i], new_states[i], store_sem.at[i])
        copy.start()
        stores.append(copy)
    for c in range(PIECES):
        for k in order[:-1]:
            gz_copies[k, c].wait_recv()
            forward(k, c)
        if c + DEPTH < PIECES:
            spread(c + DEPTH)
    own.wait()
    for copy in stores:
        copy.wait()
    for copy in gx_copies.values():
        copy.wait_recv()
    for copy in sends:
        copy.wait_send()


def finish(rows, *refs):
    sources, targets, sem = refs[:10], refs[10:22], refs[22]
    copies = []
    for g in range(3):
        start = sum(rows[:g])
        copies.append((sources[9].at[:, :, start : start + rows[g]], targets[9 + g]))
    copies += list(zip(sources[:9], targets[:9]))
    copies = [
        pltpu.make_async_copy(source, target, sem.at[i]) for i, (source, target) in enumerate(copies)
    ]
    for copy in copies:
        copy.start()
    for copy in copies:
        copy.wait()


def on_device(*arguments):
    shards, sections, tensors = (lax.axis_size(a) for a in ("shard", "section", "tensor"))
    grads, states = arguments[:3], arguments[3:]
    batches, _, width = grads[0].shape
    rows = [states[g].shape[0] for g in range(3)]
    height = sum(rows)
    entries = sum(gradient.shape[1] * width * tensors for gradient in grads)
    ceiling = clip_rms * math.sqrt(entries)
    grads = [
        gradient.reshape(batches, shards, sections, rows[g], width) for g, gradient in enumerate(grads)
    ]
    n_group = shards * sections - 1
    dma = pltpu.SemaphoreType.DMA
    scratch = (
        [pltpu.VMEM(gradient.shape, jnp.bfloat16) for gradient in grads]
        + [pltpu.VMEM(state.shape, jnp.float32) for state in states]
        + [pltpu.VMEM(state.shape, jnp.float32) for state in states]
        + [
            pltpu.VMEM((shards - 1, sections, height, width), WIRE),
            pltpu.VMEM((shards - 1, sections, height, width), WIRE),
            pltpu.VMEM((sections - 1, height, width), WIRE),
            pltpu.VMEM((sections - 1, height, width), WIRE),
            pltpu.VMEM((height, width), jnp.float32),
            pltpu.VMEM((height, width), jnp.bfloat16),
            pltpu.VMEM((8, 128), jnp.float32),
            pltpu.VMEM((n_group, 8, 128), jnp.float32),
            pltpu.VMEM((8, 128), jnp.float32),
            pltpu.VMEM((tensors - 1, 8, 128), jnp.float32),
            dma((shards, 3)),
            dma((9,)),
            dma((9,)),
            dma,
            dma((shards - 1, sections)),
            dma((shards - 1, sections)),
            dma((sections - 1,)),
            dma((sections - 1,)),
            dma((n_group,)),
            dma((n_group,)),
            dma((tensors - 1,)),
            dma((tensors - 1,)),
            dma((sections - 1, PIECES)),
            dma((sections - 1, PIECES)),
            dma((shards - 1, sections, PIECES)),
            dma((shards - 1, sections, PIECES)),
        ]
    )
    results = pl.pallas_call(
        functools.partial(kernel, (shards, sections, tensors), rows, batches, ceiling),
        out_shape=[pltpu.VMEM(state.shape, jnp.float32) for state in states]
        + [pltpu.VMEM((shards, sections, height, width), jnp.bfloat16)],
        in_specs=[pl.BlockSpec(memory_space=pltpu.HBM)] * 12,
        out_specs=[pl.BlockSpec(memory_space=pltpu.VMEM)] * 10,
        scratch_shapes=scratch,
        compiler_params=pltpu.CompilerParams(
            collective_id=0, has_side_effects=True, vmem_limit_bytes=VMEM_LIMIT
        ),
    )(*grads, *states)
    full = [
        jax.ShapeDtypeStruct((shards, sections, rows[g], width), jnp.bfloat16) for g in range(3)
    ]
    finished = pl.pallas_call(
        functools.partial(finish, rows),
        out_shape=[jax.ShapeDtypeStruct(state.shape, jnp.float32) for state in states] + full,
        in_specs=[pl.BlockSpec(memory_space=pl.ANY)] * 10,
        out_specs=[pl.BlockSpec(memory_space=pltpu.HBM)] * 12,
        scratch_shapes=[dma((12,))],
        compiler_params=pltpu.CompilerParams(vmem_limit_bytes=4 * 1024 * 1024),
    )(*results)
    weights = [part.reshape(-1, width) for part in finished[9:]]
    return (*finished[:9], *weights)


def solution(mesh):
    grad = P(("shard", "section"), None, "tensor")
    state = P(("shard", "section"), "tensor")
    return jax.shard_map(
        on_device,
        mesh=mesh,
        in_specs=(grad,) * 3 + (state,) * 9,
        out_specs=(state,) * 9 + (P(None, "tensor"),) * 3,
        check_vma=False,
    )
```
